512 devices in a mesh: grp: 16 (over z), seq: 32 (over y, x, core).
Axes of the slice: x: 4, y: 4, z: 16, core: 2. Of those that a mesh axis runs over, the one named last changes fastest.
Arguments:
- frames: bfloat16 [131072, 1024], P(('grp', 'seq')), parts along dimension 0, may hold values from -6 to 6
- w_qkv: bfloat16 [1024, 3072], P(None, 'seq'), may hold values from -2 to 2
- w_out: bfloat16 [1024, 1024], replicated, may hold values from -0.75 to 0.75
- dw_kernel: float32 [31, 1024], replicated, may hold values from -1 to 1
- conv_gain: float32 [1024], replicated, may hold values from 0.5 to 2
- conv_bias: float32 [1024], replicated, may hold values from -3 to 3
- rec_ids: int32 [131072], P('grp'), parts along dimension 0, may hold values from 0 to 7, never falling along the last dimension, each value on 1 to 2048 neighbouring positions
- left_spans: int32 [1024], P('grp'), parts along dimension 0, may hold values from 0 to 2, as said below
Outputs:
- block_out: bfloat16 [131072, 1024], P(('grp', 'seq')), parts along dimension 0
The draws below stay inside these ranges and needn't reach their ends.
There are 16 independent parts, one for each index of `grp`. The reference program is written for one: setup_inputs(seed, part) draws one part's arguments, and reference() takes and returns one part's arrays. A program takes and returns all parts, laid end to end along the dimension named above; an argument that names none is the same for every part. Nothing has to cross between parts.
Inputs may be any that keep to these rules, and one draw needn't show every extreme that they name: `left_spans`: each entry is 0 to 2; at least one span has 2 and at least one has 0.
All inputs are finite; a program needn't handle non-finite values.
Results may differ from the reference program's by a relative error of at most 0.0064.
Values may be sent and summed in bfloat16 or wider, within the bound.
A program may use at most 64 MiB of HBM per device.

```python
import math
import jax
import jax.numpy as jnp
import numpy as np
from jax import lax

D = 1024
HEADS = 16
HEAD = 64
KERNEL = 31
HALF = 15
SPAN = 128
LMAX = 2
FRAMES = 8192
NCH = 64
RECS = 8
REC_MOST = 2048


def draw_w_qkv(key, part):
    base = jax.random.normal(key, (D, 3 * D), jnp.float32) / D ** 0.5
    return jnp.clip(base, -2.0, 2.0).astype(jnp.bfloat16)


def draw_left_spans(key, part):
    counts = jax.random.randint(key, (NCH,), 0, LMAX + 1)
    spot = jax.random.randint(jax.random.fold_in(key, 21), (), 0, NCH)
    offset = jax.random.randint(jax.random.fold_in(key, 22), (), 1, NCH)
    other = (spot + offset) % NCH
    counts = counts.at[other].set(0)
    return counts.at[spot].set(LMAX).astype(jnp.int32)


def block_levels(stream_key, shape, pieces, least, high):
    factor_of = 1.0
    for dim, parts in pieces:
        heights = jax.random.uniform(jax.random.fold_in(jax.random.fold_in(stream_key, 6), dim), (parts,), jnp.float32, least / len(pieces), high / len(pieces))
        factor_of = factor_of * jnp.repeat(jnp.exp(heights), shape[dim] // parts).reshape((-1,) + (1,) * (len(shape) - 1 - dim))
    return factor_of


def length_profile(count, total, most, lean):
    weights = [(1 << 20) // math.isqrt(rank ** lean) + 1 for rank in range(2, count + 1)]
    spare, given = total - most - (count - 1), [1] * (count - 1)
    while spare > 0:
        candidates = [i for i in range(count - 1) if given[i] < most]
        mass, remaining = sum([weights[i] for i in candidates]), spare
        for i in candidates:
            extra = min(most - given[i], max(1, remaining * weights[i] // mass), spare)
            given[i] = given[i] + extra
            spare = spare - extra
    return np.array([most] + given)


def uneven(rng, amount, total, most, lean):
    if amount == 2:
        one = jax.random.randint(rng, (), max(1, total - most), min(most, total - 1) + 1)
        return jnp.stack([one, total - one])
    sizes = jnp.asarray(length_profile(amount, total, most, lean), jnp.int32)
    couples = (amount - 1) // 2
    source_of, receiver = sizes[1:1 + 2 * couples:2], sizes[2:2 + 2 * couples:2]
    margin = jnp.minimum(source_of - 1, most - receiver)
    moved = jax.random.randint(jax.random.fold_in(rng, 1), (couples,), 0, 1 << 20) % (margin + 1)
    sizes = sizes.at[1:1 + 2 * couples:2].set(source_of - moved).at[2:2 + 2 * couples:2].set(receiver + moved)
    return sizes[jax.random.permutation(jax.random.fold_in(rng, 2), amount)]


def scatter_about(key, extent, scale, most, pieces=(), kind=jnp.bfloat16):
    loudness = block_levels(key, extent, pieces, -0.22, 0.18) if pieces else 1.0
    entries = jax.random.normal(key, extent, jnp.float32) * scale * loudness
    return jnp.minimum(jnp.maximum(entries, -most), most).astype(kind)


def setup_inputs(seed: int = 0, part: int = 0) -> dict:
    seeds = jax.random.split(jax.random.key(seed), 9)
    own_keys = jax.random.split(jax.random.fold_in(seeds[8], part), 9)
    return {
        "frames": scatter_about(own_keys[0], (FRAMES, D), 1.0, 6.0, ((0, 32),)),
        "w_qkv": draw_w_qkv(jax.random.fold_in(seeds[8], 71), part),
        "w_out": scatter_about(seeds[2], (D, D), HEAD ** -0.5, 0.75),
        "dw_kernel": scatter_about(seeds[3], (KERNEL, D), KERNEL ** -0.5, 1.0, (), jnp.float32),
        "conv_gain": jnp.clip(jnp.exp(jax.random.uniform(seeds[4], (D,), jnp.float32, math.log(0.5), math.log(2.0))), 0.5, 2.0),
        "conv_bias": scatter_about(seeds[5], (D,), 0.5, 3.0, (), jnp.float32),
        "rec_ids": jnp.searchsorted(jnp.cumsum(uneven(own_keys[6], RECS, FRAMES, REC_MOST, 0)), jnp.arange(FRAMES), side="right").astype(jnp.int32),
        "left_spans": draw_left_spans(jax.random.fold_in(jax.random.fold_in(seeds[8], part), 71), part),
    }


def layer_norm(values):
    centred = values - lax.optimization_barrier(jnp.mean(values, axis=-1, keepdims=True))
    return centred / jnp.sqrt(lax.optimization_barrier(jnp.mean(centred * centred, axis=-1, keepdims=True)) + 1e-05)

def reference(frames, w_qkv, w_out, dw_kernel, conv_gain, conv_bias, rec_ids, left_spans):
    inputs = frames.astype(jnp.float32)
    normed = layer_norm(inputs).astype(jnp.bfloat16)
    qkv = jnp.dot(normed, w_qkv, preferred_element_type=jnp.float32).astype(jnp.bfloat16)
    queries = qkv[:, :D].reshape(FRAMES, HEADS, HEAD)
    context = LMAX * SPAN
    width = context + SPAN
    keys = jnp.pad(qkv[:, D:2 * D], ((context, 0), (0, 0))).reshape(FRAMES + context, HEADS, HEAD)
    values = jnp.pad(qkv[:, 2 * D:], ((context, 0), (0, 0))).reshape(FRAMES + context, HEADS, HEAD)
    rec_padded = jnp.pad(rec_ids, (context, 0), constant_values=-1)
    scale = 1.0 / HEAD ** 0.5

    def one_span(span):
        first = (span * SPAN).astype(jnp.int32)
        q_block = lax.dynamic_slice_in_dim(queries, first, SPAN, 0).astype(jnp.float32)
        k_block = lax.dynamic_slice_in_dim(keys, first, width, 0).astype(jnp.float32)
        v_block = lax.dynamic_slice_in_dim(values, first, width, 0).astype(jnp.float32)
        rec_query = lax.dynamic_slice_in_dim(rec_ids, first, SPAN, 0)
        rec_key = lax.dynamic_slice_in_dim(rec_padded, first, width, 0)
        key_pos = first - context + jnp.arange(width, dtype=jnp.int32)
        key_span = jnp.floor_divide(key_pos, SPAN)
        lowest = span - left_spans[span]
        allowed = (key_pos >= 0)[None, :] & (key_span >= lowest)[None, :] & (rec_key[None, :] == rec_query[:, None])
        scores = jnp.einsum('qhd,khd->hqk', q_block, k_block) * scale
        scores = jnp.where(allowed[None], scores, -1e+30)
        top = lax.optimization_barrier(jnp.max(scores, axis=-1, keepdims=True))
        expo = jnp.where(allowed[None], jnp.exp(scores - top), 0.0)
        weights = (expo / lax.optimization_barrier(jnp.sum(expo, axis=-1, keepdims=True))).astype(jnp.bfloat16)
        out = jnp.einsum('hqk,khd->qhd', weights.astype(jnp.float32), v_block)
        return out.reshape(SPAN, D).astype(jnp.bfloat16)
    attended = lax.map(one_span, jnp.arange(NCH, dtype=jnp.int32)).reshape(FRAMES, D)
    mid = (inputs + jnp.dot(attended, w_out, preferred_element_type=jnp.float32)).astype(jnp.bfloat16)
    cnormed = layer_norm(mid.astype(jnp.float32)).astype(jnp.bfloat16)
    padded = jnp.pad(cnormed.astype(jnp.float32), ((HALF, HALF), (0, 0)))
    rec_conv = jnp.pad(rec_ids, (HALF, HALF), constant_values=-1)
    conv = jnp.zeros((FRAMES, D), jnp.float32)
    for tap in range(KERNEL):
        same = (rec_conv[tap:tap + FRAMES] == rec_ids)[:, None]
        conv = conv + jnp.where(same, dw_kernel[tap][None, :] * padded[tap:tap + FRAMES], 0.0)
    shifted = conv_gain[None, :] * conv + conv_bias[None, :]
    return (mid.astype(jnp.float32) + shifted * jax.nn.sigmoid(shifted)).astype(jnp.bfloat16)
```

```python
import functools

import jax
import jax.numpy as jnp
from jax import lax
from jax.experimental import pallas as pl
from jax.experimental.pallas import tpu as pltpu
from jax.sharding import PartitionSpec as P

MESH = pl.DeviceIdType.MESH
D = 1024
ROWS = 256
SHARD = 96
SUB = 32
TAPS = 31
HALF = 15
NB = D // 128
LOG2E = 1.4426950408889634

ARRIVALS = (
    (-1, 0, "B"), (0, -1, "B"), (0, 1, "B"), (1, 0, "B"), (-1, 0, "A"), (0, -1, "A"), (0, 1, "A"), (1, 0, "A"),
    (2, 0, "B"), (-1, 0, "C"), (0, -1, "C"), (0, 1, "C"), (1, 0, "C"), (-1, 1, "B"), (1, 1, "B"), (0, 2, "B"),
    (2, 0, "A"), (2, 0, "C"), (-1, 1, "A"), (1, 1, "A"), (-1, -1, "B"), (1, -1, "B"), (-1, 1, "C"), (1, 1, "C"),
    (0, 2, "C"), (2, 1, "B"), (0, 2, "A"), (-1, 2, "B"), (-1, -1, "A"), (1, 2, "B"), (2, 1, "A"), (1, -1, "A"),
    (1, -1, "C"), (-1, -1, "C"), (2, -1, "B"), (2, 1, "C"), (2, 2, "B"), (2, -1, "A"), (-1, 2, "C"), (1, 2, "C"),
    (-1, 2, "A"), (1, 2, "A"), (2, -1, "C"), (2, 2, "C"), (2, 2, "A"),
)
RECV = {key: i for i, key in enumerate(ARRIVALS)}
RELAY = {"A": 1, "B": -1}
SHARDS = tuple((d1, d2) for d1 in (0, 1, -1, 2) for d2 in (0, 1, -1, 2))
PAIR = {}
for _d in SHARDS:
    if _d == (0, 0):
        PAIR[_d + ("own",)] = len(PAIR)
    else:
        PAIR[_d + ("AB",)] = len(PAIR)
        PAIR[_d + ("C",)] = len(PAIR)
ZSIGN = {}
for _key in ARRIVALS:
    if _key[2] == "B":
        ZSIGN[_key[:2]] = 1 if len(ZSIGN) % 2 == 0 else -1
NSEND = 160


def layer_norm(values):
    centred = values - jnp.mean(values, axis=-1, keepdims=True)
    return centred / jnp.sqrt(jnp.mean(centred * centred, axis=-1, keepdims=True) + 1e-05)


def kernel(
    x_hbm, w_hbm, wo_hbm, dw_ref, gain_ref, bias_ref, rec_ref, left_ref, out_ref,
    wbuf, xown, xprev, normed, qkv, wo, attended, bias_s, cbuf, cedge, halo, rcol, xs,
    loc_sem, send_sem, recv_sem, pair_sem, frame_sem, halo_sem,
):
    seq = lax.axis_index("seq")
    grp = lax.axis_index("grp")
    k = lax.rem(seq, 2)
    chip = seq // 2
    x, y = lax.rem(chip, 4), chip // 4
    i1 = x + k * (y - x)
    i2 = y + k * (x - y)
    st1 = 2 + 6 * k
    st2 = 8 - 6 * k
    par = lax.rem(grp, 2)
    other = 1 - k

    def seq_at(d1, d2):
        return lax.rem(i1 + d1 + 4, 4) * st1 + lax.rem(i2 + d2 + 4, 4) * st2 + k

    def pair_at(d1, d2):
        return lax.rem(i2 + d1 + 4, 4) * st2 + lax.rem(i1 + d2 + 4, 4) * st1 + other

    start_of = {"A": SUB, "B": 2 * SUB * par, "C": 2 * SUB * (1 - par), "AB": SUB * par, "own": 0}
    size_of = {"A": SUB, "B": SUB, "C": SUB, "AB": 2 * SUB, "own": SHARD}

    def rows_of(owner, piece):
        return pl.ds(pl.multiple_of(owner * SHARD + start_of[piece], SUB), size_of[piece])

    nxt, prv = lax.rem(seq + 1, 32), lax.rem(seq + 31, 32)
    partner = seq + 1 - 2 * k
    far = lax.rem(seq + 31 + 2 * k, 32)
    ax1 = {1: seq_at(1, 0), -1: seq_at(-1, 0)}
    ax2 = {1: seq_at(0, 1), -1: seq_at(0, -1)}
    zto = {1: lax.rem(grp + 1 + 14 * k, 16), -1: lax.rem(grp + 15 - 14 * k, 16)}
    sends = []

    local = [
        pltpu.make_async_copy(x_hbm, xown, loc_sem.at[0]),
        pltpu.make_async_copy(wo_hbm, wo, loc_sem.at[1]),
        pltpu.make_async_copy(
            w_hbm, wbuf.at[pl.ds(pl.multiple_of(seq * SHARD, SUB), SHARD)], loc_sem.at[2]
        ),
    ]
    for copy in local:
        copy.start()

    barrier = pltpu.get_barrier_semaphore()
    for target in (ax1[1], ax1[-1], ax2[1], ax2[-1], partner, far):
        pl.semaphore_signal(barrier, inc=1, device_id={"seq": target}, device_id_type=MESH)
    for sign in (1, -1):
        pl.semaphore_signal(barrier, inc=1, device_id={"grp": zto[sign]}, device_id_type=MESH)
    pl.semaphore_wait(barrier, 8)

    def send(src, dst, sem, where):
        copy = pltpu.make_async_remote_copy(
            src_ref=src, dst_ref=dst, send_sem=send_sem.at[len(sends)], recv_sem=sem, device_id=where,
            device_id_type=MESH,
        )
        copy.start()
        sends.append(copy)

    def forward(rel, piece, where, key):
        rows = rows_of(seq_at(*rel), piece)
        send(wbuf.at[rows], wbuf.at[rows], recv_sem.at[RECV[key]], where)

    def to_pair(rel, piece):
        rows = rows_of(seq_at(*rel), piece)
        send(wbuf.at[rows], wbuf.at[rows], pair_sem.at[PAIR[rel + (piece,)]], {"seq": partner})

    for piece in ("B", "A"):
        source = w_hbm.at[pl.ds(pl.multiple_of(start_of[piece] + 0 * seq, SUB), SUB)]
        target = wbuf.at[rows_of(seq, piece)]
        for sign in (1, -1):
            send(source, target, recv_sem.at[RECV[-sign, 0, piece]], {"seq": ax1[sign]})
        for sign in (1, -1):
            send(source, target, recv_sem.at[RECV[0, -sign, piece]], {"seq": ax2[sign]})
    own_rows = pl.ds(pl.multiple_of(seq * SHARD, SUB), SHARD)
    send(w_hbm, wbuf.at[own_rows], pair_sem.at[PAIR[0, 0, "own"]], {"seq": partner})
    for part in range(4):
        rows = pl.ds(part * 64, 64)
        send(x_hbm.at[rows], xprev.at[rows], frame_sem.at[part], {"seq": nxt})

    local[0].wait()
    normed[ROWS:] = layer_norm(xown[...].astype(jnp.float32)).astype(jnp.bfloat16)
    first = 2 * seq
    spans = [
        rec_ref[pl.ds(lax.rem(first + o + 64, 64), 1), :] for o in (-2, -1, 0, 1, 2)
    ]
    missing = jnp.full((1, 128), -1, jnp.int32)
    spans[0] = jnp.where(seq > 0, spans[0], missing)
    spans[1] = jnp.where(seq > 0, spans[1], missing)
    spans[4] = jnp.where(seq < 31, spans[4], missing)
    cols = [jnp.transpose(jnp.broadcast_to(row, (128, 128))) for row in spans]
    rcol[0:16] = cols[1][112:128]
    rcol[16:144] = cols[2]
    rcol[144:272] = cols[3]
    rcol[272:288] = cols[4][0:16]
    for span in range(2):
        left = left_ref[first + span]
        for block in range(3):
            keys = spans[span + block]
            if block < 2:
                keys = jnp.where(left >= 2 - block, keys, missing)
            same = jnp.broadcast_to(keys, (128, 128)) == cols[span + 2]
            bias_s[span, :, block * 128 : block * 128 + 128] = jnp.where(same, 0.0, -1e30)

    arrived = set()
    for key in ARRIVALS:
        d1, d2, piece = key
        rel = (d1, d2)
        rows = rows_of(seq_at(d1, d2), piece)
        pltpu.make_async_copy(wbuf.at[rows], wbuf.at[rows], recv_sem.at[RECV[key]]).wait()
        arrived.add(key)
        if piece == "C":
            to_pair(rel, "C")
            continue
        if d2 == 0:
            if d1 == -RELAY[piece]:
                forward(rel, piece, {"seq": ax1[RELAY[piece]]}, (2, 0, piece))
            for sign in (1, -1):
                forward(rel, piece, {"seq": ax2[sign]}, (d1, -sign, piece))
        elif d2 == -RELAY[piece]:
            forward(rel, piece, {"seq": ax2[RELAY[piece]]}, (d1, 2, piece))
        if piece == "B":
            forward(rel, piece, {"grp": zto[ZSIGN[rel]]}, rel + ("C",))
        if rel + ("A",) in arrived and rel + ("B",) in arrived:
            to_pair(rel, "AB")

    for part in range(4):
        rows = pl.ds(part * 64, 64)
        pltpu.make_async_copy(xprev.at[rows], xprev.at[rows], frame_sem.at[part]).wait()
    normed[:ROWS] = layer_norm(xprev[...].astype(jnp.float32)).astype(jnp.bfloat16)
    for d1, d2, piece in PAIR:
        rows = rows_of(pair_at(d1, d2), piece)
        pltpu.make_async_copy(wbuf.at[rows], wbuf.at[rows], pair_sem.at[PAIR[d1, d2, piece]]).wait()
    local[2].wait()

    @pl.loop(0, 12)
    def _(block):
        rows = pl.ds(pl.multiple_of(block * 256, 256), 256)
        part = lax.dot_general(
            normed[...], wbuf[rows, :], (((1,), (1,)), ((), ())), preferred_element_type=jnp.float32
        ).astype(jnp.bfloat16)
        qkv[2 * block] = part[:, :128]
        qkv[2 * block + 1] = part[:, 128:]

    lane = lax.broadcasted_iota(jnp.int32, (128, 128), 1)
    low = lane < 64

    @pl.loop(0, NB)
    def _(pair):
        for span in range(2):
            q = qkv[pair, ROWS + span * 128 : ROWS + span * 128 + 128, :]
            keys = qkv[NB + pair, span * 128 : span * 128 + 384, :]
            values = qkv[2 * NB + pair, span * 128 : span * 128 + 384, :]
            zero = jnp.zeros_like(q)
            both = jnp.concatenate([jnp.where(low, q, zero), jnp.where(low, zero, q)], axis=0)
            scores = lax.dot_general(
                both, keys, (((1,), (1,)), ((), ())), preferred_element_type=jnp.float32
            )
            mask = bias_s[span]
            scores = scores * (0.125 * LOG2E) + jnp.concatenate([mask, mask], axis=0)
            expo = jnp.exp2(scores - jnp.max(scores, axis=-1, keepdims=True))
            total = jnp.sum(expo, axis=-1, keepdims=True)
            got = jnp.dot(expo.astype(jnp.bfloat16), values, preferred_element_type=jnp.float32)
            got = got / total
            attended[pair, span * 128 : span * 128 + 128, :] = jnp.where(
                low, got[:128], got[128:]
            ).astype(jnp.bfloat16)

    local[1].wait()
    flat = jnp.concatenate([attended[i] for i in range(NB)], axis=1)
    for part in range(4):
        lanes = slice(part * 256, part * 256 + 256)
        cbuf[:, lanes] = (
            xown[:, lanes].astype(jnp.float32)
            + jnp.dot(flat, wo[:, lanes], preferred_element_type=jnp.float32)
        ).astype(jnp.bfloat16)
    cnormed = layer_norm(cbuf[...].astype(jnp.float32)).astype(jnp.bfloat16)
    cedge[0] = cnormed[:16]
    cedge[1] = cnormed[ROWS - 16 :]
    send(cedge.at[0], halo.at[1], halo_sem.at[1], {"seq": prv})
    send(cedge.at[1], halo.at[0], halo_sem.at[0], {"seq": nxt})
    wide = cnormed.astype(jnp.float32)
    for i in range(NB):
        xs[i, 16 : 16 + ROWS, :] = wide[:, i * 128 : i * 128 + 128]
    for side in range(2):
        pltpu.make_async_copy(halo.at[side], halo.at[side], halo_sem.at[side]).wait()
        wide_halo = halo[side].astype(jnp.float32)
        for i in range(NB):
            xs[i, side * (ROWS + 16) : side * (ROWS + 16) + 16, :] = wide_halo[:, i * 128 : i * 128 + 128]

    tile = 16

    @pl.loop(0, ROWS // tile)
    def _(step):
        base = pl.multiple_of(step * tile, tile)
        own = rcol[pl.ds(base + 16, tile), :]
        sums = [jnp.zeros((tile, 128), jnp.float32) for _ in range(NB)]
        for tap in range(TAPS):
            same = rcol[pl.ds(base + tap + 1, tile), :] == own
            for i in range(NB):
                term = dw_ref[tap : tap + 1, i * 128 : i * 128 + 128] * xs[i, pl.ds(base + tap + 1, tile), :]
                sums[i] = sums[i] + jnp.where(same, term, 0.0)
        for i in range(NB):
            lanes = slice(i * 128, i * 128 + 128)
            z = gain_ref[:, lanes] * sums[i] + bias_ref[:, lanes]
            mid = cbuf[pl.ds(base, tile), lanes].astype(jnp.float32)
            out_ref[pl.ds(base, tile), lanes] = (mid + z * jax.nn.sigmoid(z)).astype(jnp.bfloat16)

    for copy in sends:
        copy.wait_send()


def on_device(frames, w_qkv, w_out, dw_kernel, conv_gain, conv_bias, rec_ids, left_spans):
    vmem = pl.BlockSpec(memory_space=pltpu.VMEM)
    anyspace = pl.BlockSpec(memory_space=pl.ANY)
    bf = jnp.bfloat16
    return pl.pallas_call(
        kernel,
        out_shape=jax.ShapeDtypeStruct((ROWS, D), bf),
        in_specs=[anyspace, anyspace, anyspace, vmem, vmem, vmem, vmem,
                  pl.BlockSpec(memory_space=pltpu.SMEM)],
        out_specs=vmem,
        scratch_shapes=[
            pltpu.VMEM((3 * D, D), bf),
            pltpu.VMEM((ROWS, D), bf),
            pltpu.VMEM((ROWS, D), bf),
            pltpu.VMEM((2 * ROWS, D), bf),
            pltpu.VMEM((3 * NB, 2 * ROWS, 128), bf),
            pltpu.VMEM((D, D), bf),
            pltpu.VMEM((NB, ROWS, 128), bf),
            pltpu.VMEM((2, 128, 384), jnp.float32),
            pltpu.VMEM((ROWS, D), bf),
            pltpu.VMEM((2, 16, D), bf),
            pltpu.VMEM((2, 16, D), bf),
            pltpu.VMEM((ROWS + 32, 128), jnp.int32),
            pltpu.VMEM((NB, ROWS + 32, 128), jnp.float32),
            pltpu.SemaphoreType.DMA((3,)),
            pltpu.SemaphoreType.DMA((NSEND,)),
            pltpu.SemaphoreType.DMA((len(ARRIVALS),)),
            pltpu.SemaphoreType.DMA((len(PAIR),)),
            pltpu.SemaphoreType.DMA((4,)),
            pltpu.SemaphoreType.DMA((2,)),
        ],
        compiler_params=pltpu.CompilerParams(
            collective_id=0, has_side_effects=True, vmem_limit_bytes=56 * 1024 * 1024
        ),
    )(
        frames, jnp.transpose(w_qkv), w_out, dw_kernel, conv_gain.reshape(1, D), conv_bias.reshape(1, D),
        rec_ids.reshape(64, 128), left_spans,
    )


def solution(mesh):
    in_specs = (P(("grp", "seq"), None), P(None, "seq"), P(), P(), P(), P(), P("grp"), P("grp"))
    out_specs = P(("grp", "seq"), None)
    return jax.shard_map(
        on_device, mesh=mesh, in_specs=in_specs, out_specs=out_specs, check_vma=False
    )
```

```python
import functools

import jax
import jax.numpy as jnp
from jax import lax
from jax.experimental import pallas as pl
from jax.experimental.pallas import tpu as pltpu
from jax.sharding import PartitionSpec as P

MESH = pl.DeviceIdType.MESH
D = 1024
ROWS = 256
SHARD = 96
TAPS = 31
HALF = 15
NB = D // 128
LOG2E = 1.4426950408889634

ARRIVALS = (
    (1, 0, "A"), (-1, 0, "A"), (1, 0, "C"), (-1, 0, "C"), (1, 0, "B"), (0, 1, "A"), (-1, 0, "B"), (2, 0, "A"),
    (0, -1, "A"), (0, 1, "C"), (1, -1, "A"), (0, -1, "C"), (2, 0, "C"), (-1, -1, "A"), (0, -1, "B"), (1, 1, "A"),
    (0, 1, "B"), (-1, 1, "A"), (2, 0, "B"), (1, -1, "C"), (1, 1, "C"), (-1, -1, "C"), (-1, 1, "C"), (2, 1, "A"),
    (0, 2, "C"), (1, 1, "B"), (2, 1, "C"), (-1, 1, "B"), (1, -1, "B"), (0, 2, "B"), (2, -1, "A"), (1, 2, "C"),
    (-1, -1, "B"), (0, 2, "A"), (1, 2, "A"), (2, -1, "C"), (2, 1, "B"), (-1, 2, "C"), (-1, 2, "A"), (1, 2, "B"),
    (-1, 2, "B"), (2, -1, "B"), (2, 2, "A"), (2, 2, "C"), (2, 2, "B"),
)
RECV = {key: i for i, key in enumerate(ARRIVALS)}
START = {"A": 0, "C": 16, "B": 48, "AC": 0, "own": 0}
SIZE = {"A": 16, "C": 32, "B": 48, "AC": 48, "own": SHARD}
RELAY = {"A": 1, "B": -1}
SHARDS = tuple((d1, d2) for d1 in (0, 1, -1, 2) for d2 in (0, 1, -1, 2))
PAIR = {}
for _d in SHARDS:
    for _piece in ("own",) if _d == (0, 0) else ("AC", "B"):
        PAIR[_d + (_piece,)] = len(PAIR)
FRAME_PARTS = {0: 0, 6: 1, 12: 2, 18: 3}
GROUPS = {37: 0, 42: 1, 43: -1}
NSEND = 128


def layer_norm(values):
    centred = values - jnp.mean(values, axis=-1, keepdims=True)
    return centred / jnp.sqrt(jnp.mean(centred * centred, axis=-1, keepdims=True) + 1e-05)


def kernel(
    x_hbm, w_hbm, wo_hbm, dw_ref, gain_ref, bias_ref, rec_ref, left_ref, out_ref,
    wbuf, xown, xprev, normed, qkv, wo, attended, bias_s, cbuf, cedge, halo, rcol, xs,
    loc_sem, send_sem, recv_sem, pair_sem, frame_sem, halo_sem,
):
    seq = lax.axis_index("seq")
    k = lax.rem(seq, 2)
    chip = seq // 2
    x, y = lax.rem(chip, 4), chip // 4
    i1 = x + k * (y - x)
    i2 = y + k * (x - y)
    st1 = 2 + 6 * k
    st2 = 8 - 6 * k
    other = 1 - k
    turn1 = 2 * k - 1
    turn2 = 1 - 2 * k

    def seq_at(d1, d2):
        return lax.rem(i1 + d1 + 4, 4) * st1 + lax.rem(i2 + d2 + 4, 4) * st2 + k

    def pair_at(d1, d2):
        return lax.rem(i2 + d1 + 4, 4) * st2 + lax.rem(i1 + d2 + 4, 4) * st1 + other

    def rows_of(owner, piece):
        return pl.ds(pl.multiple_of(owner * SHARD + START[piece], 16), SIZE[piece])

    nxt, prv = lax.rem(seq + 1, 32), lax.rem(seq + 31, 32)
    partner = seq + 1 - 2 * k
    far = lax.rem(seq + 31 + 2 * k, 32)
    ax1 = {1: seq_at(1, 0), -1: seq_at(-1, 0)}
    ax2 = {1: seq_at(0, 1), -1: seq_at(0, -1)}
    sends = []

    local = [
        pltpu.make_async_copy(x_hbm, xown, loc_sem.at[0]),
        pltpu.make_async_copy(wo_hbm, wo, loc_sem.at[1]),
        pltpu.make_async_copy(
            w_hbm, wbuf.at[pl.ds(pl.multiple_of(seq * SHARD, 16), SHARD)], loc_sem.at[2]
        ),
    ]
    for copy in local:
        copy.start()

    barrier = pltpu.get_barrier_semaphore()
    for target in (ax1[1], ax1[-1], ax2[1], ax2[-1], partner, far):
        pl.semaphore_signal(barrier, inc=1, device_id={"seq": target}, device_id_type=MESH)
    pl.semaphore_wait(barrier, 6)

    def send(src, dst, sem, where):
        copy = pltpu.make_async_remote_copy(
            src_ref=src, dst_ref=dst, send_sem=send_sem.at[len(sends)], recv_sem=sem, device_id=where,
            device_id_type=MESH,
        )
        copy.start()
        sends.append(copy)

    def forward(owner, piece, where, key):
        rows = rows_of(owner, piece)
        send(wbuf.at[rows], wbuf.at[rows], recv_sem.at[RECV[key]], {"seq": where})

    def to_pair(rel, piece):
        rows = rows_of(seq_at(*rel), piece)
        send(wbuf.at[rows], wbuf.at[rows], pair_sem.at[PAIR[rel + (piece,)]], {"seq": partner})

    def send_frames(part):
        rows = pl.ds(part * 64, 64)
        send(x_hbm.at[rows], xprev.at[rows], frame_sem.at[part], {"seq": nxt})

    for piece in ("A", "C", "B"):
        source = w_hbm.at[pl.ds(START[piece], SIZE[piece])]
        target = wbuf.at[rows_of(seq, piece)]
        for sign in (1, -1):
            send(source, target, recv_sem.at[RECV[-sign, 0, piece]], {"seq": ax1[sign]})
        for sign in (1, -1):
            send(source, target, recv_sem.at[RECV[0, -sign, piece]], {"seq": ax2[sign]})
    own_rows = pl.ds(pl.multiple_of(seq * SHARD, 16), SHARD)
    send(w_hbm, wbuf.at[own_rows], pair_sem.at[PAIR[0, 0, "own"]], {"seq": partner})
    send_frames(FRAME_PARTS[0])

    local[0].wait()
    normed[ROWS:] = layer_norm(xown[...].astype(jnp.float32)).astype(jnp.bfloat16)
    first = 2 * seq
    spans = [
        rec_ref[pl.ds(lax.rem(first + o + 64, 64), 1), :] for o in (-2, -1, 0, 1, 2)
    ]
    missing = jnp.full((1, 128), -1, jnp.int32)
    spans[0] = jnp.where(seq > 0, spans[0], missing)
    spans[1] = jnp.where(seq > 0, spans[1], missing)
    spans[4] = jnp.where(seq < 31, spans[4], missing)
    cols = [jnp.transpose(jnp.broadcast_to(row, (128, 128))) for row in spans]
    rcol[0:16] = cols[1][112:128]
    rcol[16:144] = cols[2]
    rcol[144:272] = cols[3]
    rcol[272:288] = cols[4][0:16]
    for span in range(2):
        left = left_ref[first + span]
        for block in range(3):
            keys = spans[span + block]
            if block < 2:
                keys = jnp.where(left >= 2 - block, keys, missing)
            same = jnp.broadcast_to(keys, (128, 128)) == cols[span + 2]
            bias_s[span, :, block * 128 : block * 128 + 128] = jnp.where(same, 0.0, -1e30)

    taken = set()

    def from_pair(shards):
        for key in PAIR:
            if key[:2] in shards and key not in taken:
                taken.add(key)
                rows = rows_of(pair_at(key[0], key[1]), key[2])
                pltpu.make_async_copy(wbuf.at[rows], wbuf.at[rows], pair_sem.at[PAIR[key]]).wait()

    def project(dy):
        from_pair([d for d in SHARDS if dy in d])
        first_block = 3 * lax.rem(y + dy + 4, 4)

        @pl.loop(0, 3)
        def _(j):
            block = first_block + j
            rows = pl.ds(pl.multiple_of(block * 256, 256), 256)

            @pl.when(block < 4)
            def _():
                part = lax.dot_general(
                    normed[ROWS:, :], wbuf[rows, :], (((1,), (1,)), ((), ())), preferred_element_type=jnp.float32
                ).astype(jnp.bfloat16)
                qkv[2 * block, ROWS:, :] = part[:, :128]
                qkv[2 * block + 1, ROWS:, :] = part[:, 128:]

            @pl.when(block >= 4)
            def _():
                part = lax.dot_general(
                    normed[...], wbuf[rows, :], (((1,), (1,)), ((), ())), preferred_element_type=jnp.float32
                ).astype(jnp.bfloat16)
                qkv[2 * block] = part[:, :128]
                qkv[2 * block + 1] = part[:, 128:]

    arrived = set()
    for count, key in enumerate(ARRIVALS, 1):
        d1, d2, piece = key
        rel = (d1, d2)
        owner = seq_at(d1, d2)
        rows = rows_of(owner, piece)
        pltpu.make_async_copy(wbuf.at[rows], wbuf.at[rows], recv_sem.at[RECV[key]]).wait()
        arrived.add(key)
        if d2 == 0:
            if piece == "C":
                if {(1, 0, "C"), (-1, 0, "C")} <= arrived and d1 != 2:
                    forward(seq_at(-turn1, 0), "C", seq_at(turn1, 0), (2, 0, "C"))
            elif d1 == -RELAY[piece]:
                forward(owner, piece, ax1[RELAY[piece]], (2, 0, piece))
            for sign in (1, -1):
                forward(owner, piece, ax2[sign], (d1, -sign, piece))
        elif piece == "C":
            if {(d1, 1, "C"), (d1, -1, "C")} <= arrived and d2 != 2:
                forward(seq_at(d1, -turn2), "C", seq_at(0, turn2), (d1, 2, "C"))
        elif d2 == -RELAY[piece]:
            forward(owner, piece, ax2[RELAY[piece]], (d1, 2, piece))
        if piece == "B":
            to_pair(rel, "B")
        elif rel + ("A",) in arrived and rel + ("C",) in arrived:
            to_pair(rel, "AC")
        if count in FRAME_PARTS:
            send_frames(FRAME_PARTS[count])
        if count == 33:
            for part in range(4):
                rows = pl.ds(part * 64, 64)
                pltpu.make_async_copy(xprev.at[rows], xprev.at[rows], frame_sem.at[part]).wait()
            normed[:ROWS] = layer_norm(xprev[...].astype(jnp.float32)).astype(jnp.bfloat16)
            local[2].wait()
        if count in GROUPS:
            project(GROUPS[count])
    project(2)

    lane = lax.broadcasted_iota(jnp.int32, (128, 128), 1)
    low = lane < 64

    @pl.loop(0, NB)
    def _(pair):
        for span in range(2):
            q = qkv[pair, ROWS + span * 128 : ROWS + span * 128 + 128, :]
            keys = qkv[NB + pair, span * 128 : span * 128 + 384, :]
            values = qkv[2 * NB + pair, span * 128 : span * 128 + 384, :]
            zero = jnp.zeros_like(q)
            both = jnp.concatenate([jnp.where(low, q, zero), jnp.where(low, zero, q)], axis=0)
            scores = lax.dot_general(
                both, keys, (((1,), (1,)), ((), ())), preferred_element_type=jnp.float32
            )
            mask = bias_s[span]
            scores = scores * (0.125 * LOG2E) + jnp.concatenate([mask, mask], axis=0)
            expo = jnp.exp2(scores - jnp.max(scores, axis=-1, keepdims=True))
            total = jnp.sum(expo, axis=-1, keepdims=True)
            got = jnp.dot(expo.astype(jnp.bfloat16), values, preferred_element_type=jnp.float32)
            got = got / total
            attended[pair, span * 128 : span * 128 + 128, :] = jnp.where(
                low, got[:128], got[128:]
            ).astype(jnp.bfloat16)

    local[1].wait()
    flat = jnp.concatenate([attended[i] for i in range(NB)], axis=1)
    for part in range(4):
        lanes = slice(part * 256, part * 256 + 256)
        cbuf[:, lanes] = (
            xown[:, lanes].astype(jnp.float32)
            + jnp.dot(flat, wo[:, lanes], preferred_element_type=jnp.float32)
        ).astype(jnp.bfloat16)
    cnormed = layer_norm(cbuf[...].astype(jnp.float32)).astype(jnp.bfloat16)
    cedge[0] = cnormed[:16]
    cedge[1] = cnormed[ROWS - 16 :]
    send(cedge.at[0], halo.at[1], halo_sem.at[1], {"seq": prv})
    send(cedge.at[1], halo.at[0], halo_sem.at[0], {"seq": nxt})
    wide = cnormed.astype(jnp.float32)
    for i in range(NB):
        xs[i, 16 : 16 + ROWS, :] = wide[:, i * 128 : i * 128 + 128]
    tile = 16

    def convolve(base):
        own = rcol[pl.ds(base + 16, tile), :]
        sums = [jnp.zeros((tile, 128), jnp.float32) for _ in range(NB)]
        for tap in range(TAPS):
            same = rcol[pl.ds(base + tap + 1, tile), :] == own
            for i in range(NB):
                term = dw_ref[tap : tap + 1, i * 128 : i * 128 + 128] * xs[i, pl.ds(base + tap + 1, tile), :]
                sums[i] = sums[i] + jnp.where(same, term, 0.0)
        for i in range(NB):
            lanes = slice(i * 128, i * 128 + 128)
            z = gain_ref[:, lanes] * sums[i] + bias_ref[:, lanes]
            mid = cbuf[pl.ds(base, tile), lanes].astype(jnp.float32)
            out_ref[pl.ds(base, tile), lanes] = (mid + z * jax.nn.sigmoid(z)).astype(jnp.bfloat16)

    @pl.loop(1, ROWS // tile - 1)
    def _(step):
        convolve(pl.multiple_of(step * tile, tile))

    for side in range(2):
        pltpu.make_async_copy(halo.at[side], halo.at[side], halo_sem.at[side]).wait()
        wide_halo = halo[side].astype(jnp.float32)
        for i in range(NB):
            xs[i, side * (ROWS + 16) : side * (ROWS + 16) + 16, :] = wide_halo[:, i * 128 : i * 128 + 128]

    @pl.loop(0, 2)
    def _(step):
        convolve(pl.multiple_of(step * (ROWS - tile), tile))

    for copy in sends:
        copy.wait_send()


def on_device(frames, w_qkv, w_out, dw_kernel, conv_gain, conv_bias, rec_ids, left_spans):
    vmem = pl.BlockSpec(memory_space=pltpu.VMEM)
    anyspace = pl.BlockSpec(memory_space=pl.ANY)
    bf = jnp.bfloat16
    return pl.pallas_call(
        kernel,
        out_shape=jax.ShapeDtypeStruct((ROWS, D), bf),
        in_specs=[anyspace, anyspace, anyspace, vmem, vmem, vmem, vmem,
                  pl.BlockSpec(memory_space=pltpu.SMEM)],
        out_specs=vmem,
        scratch_shapes=[
            pltpu.VMEM((3 * D, D), bf),
            pltpu.VMEM((ROWS, D), bf),
            pltpu.VMEM((ROWS, D), bf),
            pltpu.VMEM((2 * ROWS, D), bf),
            pltpu.VMEM((3 * NB, 2 * ROWS, 128), bf),
            pltpu.VMEM((D, D), bf),
            pltpu.VMEM((NB, ROWS, 128), bf),
            pltpu.VMEM((2, 128, 384), jnp.float32),
            pltpu.VMEM((ROWS, D), bf),
            pltpu.VMEM((2, 16, D), bf),
            pltpu.VMEM((2, 16, D), bf),
            pltpu.VMEM((ROWS + 32, 128), jnp.int32),
            pltpu.VMEM((NB, ROWS + 32, 128), jnp.float32),
            pltpu.SemaphoreType.DMA((3,)),
            pltpu.SemaphoreType.DMA((NSEND,)),
            pltpu.SemaphoreType.DMA((len(ARRIVALS),)),
            pltpu.SemaphoreType.DMA((len(PAIR),)),
            pltpu.SemaphoreType.DMA((4,)),
            pltpu.SemaphoreType.DMA((2,)),
        ],
        compiler_params=pltpu.CompilerParams(
            collective_id=0, has_side_effects=True, vmem_limit_bytes=56 * 1024 * 1024
        ),
    )(
        frames, jnp.transpose(w_qkv), w_out, dw_kernel, conv_gain.reshape(1, D), conv_bias.reshape(1, D),
        rec_ids.reshape(64, 128), left_spans,
    )


def solution(mesh):
    in_specs = (P(("grp", "seq"), None), P(None, "seq"), P(), P(), P(), P(), P("grp"), P("grp"))
    out_specs = P(("grp", "seq"), None)
    return jax.shard_map(
        on_device, mesh=mesh, in_specs=in_specs, out_specs=out_specs, check_vma=False
    )
```

```python
import functools

import jax
import jax.numpy as jnp
from jax import lax
from jax.experimental import pallas as pl
from jax.experimental.pallas import tpu as pltpu
from jax.sharding import PartitionSpec as P

MESH = pl.DeviceIdType.MESH
D = 1024
ROWS = 256
SHARD = 96
TAPS = 31
HALF = 15
NB = D // 128
LOG2E = 1.4426950408889634

ARRIVALS = (
    (1, 0, "A"), (-1, 0, "A"), (1, 0, "C"), (-1, 0, "C"), (1, 0, "B"), (0, 1, "A"), (-1, 0, "B"), (2, 0, "A"),
    (0, -1, "A"), (0, 1, "C"), (1, -1, "A"), (0, -1, "C"), (2, 0, "C"), (-1, -1, "A"), (0, -1, "B"), (1, 1, "A"),
    (0, 1, "B"), (-1, 1, "A"), (2, 0, "B"), (1, -1, "C"), (1, 1, "C"), (-1, -1, "C"), (-1, 1, "C"), (2, 1, "A"),
    (0, 2, "C"), (1, 1, "B"), (2, 1, "C"), (-1, 1, "B"), (1, -1, "B"), (0, 2, "B"), (2, -1, "A"), (1, 2, "C"),
    (-1, -1, "B"), (0, 2, "A"), (1, 2, "A"), (2, -1, "C"), (2, 1, "B"), (-1, 2, "C"), (-1, 2, "A"), (1, 2, "B"),
    (-1, 2, "B"), (2, -1, "B"), (2, 2, "A"), (2, 2, "C"), (2, 2, "B"),
)
RECV = {key: i for i, key in enumerate(ARRIVALS)}
START = {"A": 0, "C": 16, "B": 48, "AC": 0, "own": 0}
SIZE = {"A": 16, "C": 32, "B": 48, "AC": 48, "own": SHARD}
RELAY = {"A": 1, "B": -1}
SHARDS = tuple((d1, d2) for d1 in (0, 1, -1, 2) for d2 in (0, 1, -1, 2))
PAIR = {}
for _d in SHARDS:
    for _piece in ("own",) if _d == (0, 0) else ("AC", "B"):
        PAIR[_d + (_piece,)] = len(PAIR)
FRAME_PARTS = {0: 0, 6: 1, 12: 2, 18: 3}
GROUPS = {37: 0, 42: 1, 43: -1}
NSEND = 128


def layer_norm(values):
    centred = values - jnp.mean(values, axis=-1, keepdims=True)
    return centred / jnp.sqrt(jnp.mean(centred * centred, axis=-1, keepdims=True) + 1e-05)


def kernel(
    x_hbm, w_hbm, wo_hbm, dw_ref, gain_ref, bias_ref, rec_ref, left_ref, out_ref,
    wbuf, xown, xprev, normed, qkv, wo, attended, bias_s, cbuf, cedge, halo, rcol, xs,
    loc_sem, send_sem, recv_sem, pair_sem, frame_sem, halo_sem,
):
    seq = lax.axis_index("seq")
    k = lax.rem(seq, 2)
    chip = seq // 2
    x, y = lax.rem(chip, 4), chip // 4
    i1 = x + k * (y - x)
    i2 = y + k * (x - y)
    st1 = 2 + 6 * k
    st2 = 8 - 6 * k
    other = 1 - k
    turn1 = 2 * k - 1
    turn2 = 1 - 2 * k

    def seq_at(d1, d2):
        return lax.rem(i1 + d1 + 4, 4) * st1 + lax.rem(i2 + d2 + 4, 4) * st2 + k

    def pair_at(d1, d2):
        return lax.rem(i2 + d1 + 4, 4) * st2 + lax.rem(i1 + d2 + 4, 4) * st1 + other

    def rows_of(owner, piece):
        return pl.ds(pl.multiple_of(owner * SHARD + START[piece], 16), SIZE[piece])

    nxt, prv = lax.rem(seq + 1, 32), lax.rem(seq + 31, 32)
    partner = seq + 1 - 2 * k
    far = lax.rem(seq + 31 + 2 * k, 32)
    ax1 = {1: seq_at(1, 0), -1: seq_at(-1, 0)}
    ax2 = {1: seq_at(0, 1), -1: seq_at(0, -1)}
    sends = []

    local = [
        pltpu.make_async_copy(x_hbm, xown, loc_sem.at[0]),
        pltpu.make_async_copy(wo_hbm, wo, loc_sem.at[1]),
        pltpu.make_async_copy(
            w_hbm, wbuf.at[pl.ds(pl.multiple_of(seq * SHARD, 16), SHARD)], loc_sem.at[2]
        ),
    ]
    for copy in local:
        copy.start()

    barrier = pltpu.get_barrier_semaphore()
    for target in (ax1[1], ax1[-1], ax2[1], ax2[-1], partner, far):
        pl.semaphore_signal(barrier, inc=1, device_id={"seq": target}, device_id_type=MESH)
    pl.semaphore_wait(barrier, 6)

    def send(src, dst, sem, where):
        copy = pltpu.make_async_remote_copy(
            src_ref=src, dst_ref=dst, send_sem=send_sem.at[len(sends)], recv_sem=sem, device_id=where,
            device_id_type=MESH,
        )
        copy.start()
        sends.append(copy)

    def forward(owner, piece, where, key):
        rows = rows_of(owner, piece)
        send(wbuf.at[rows], wbuf.at[rows], recv_sem.at[RECV[key]], {"seq": where})

    def to_pair(rel, piece):
        rows = rows_of(seq_at(*rel), piece)
        send(wbuf.at[rows], wbuf.at[rows], pair_sem.at[PAIR[rel + (piece,)]], {"seq": partner})

    def send_frames(part):
        rows = pl.ds(part * 64, 64)
        send(x_hbm.at[rows], xprev.at[rows], frame_sem.at[part], {"seq": nxt})

    for piece in ("A", "C", "B"):
        source = w_hbm.at[pl.ds(START[piece], SIZE[piece])]
        target = wbuf.at[rows_of(seq, piece)]
        for sign in (1, -1):
            send(source, target, recv_sem.at[RECV[-sign, 0, piece]], {"seq": ax1[sign]})
        for sign in (1, -1):
            send(source, target, recv_sem.at[RECV[0, -sign, piece]], {"seq": ax2[sign]})
    own_rows = pl.ds(pl.multiple_of(seq * SHARD, 16), SHARD)
    send(w_hbm, wbuf.at[own_rows], pair_sem.at[PAIR[0, 0, "own"]], {"seq": partner})
    send_frames(FRAME_PARTS[0])

    local[0].wait()
    normed[ROWS:] = layer_norm(xown[...].astype(jnp.float32)).astype(jnp.bfloat16)
    first = 2 * seq
    spans = [
        rec_ref[pl.ds(lax.rem(first + o + 64, 64), 1), :] for o in (-2, -1, 0, 1, 2)
    ]
    missing = jnp.full((1, 128), -1, jnp.int32)
    spans[0] = jnp.where(seq > 0, spans[0], missing)
    spans[1] = jnp.where(seq > 0, spans[1], missing)
    spans[4] = jnp.where(seq < 31, spans[4], missing)
    cols = [jnp.transpose(jnp.broadcast_to(row, (128, 128))) for row in spans]
    rcol[0:16] = cols[1][112:128]
    rcol[16:144] = cols[2]
    rcol[144:272] = cols[3]
    rcol[272:288] = cols[4][0:16]
    for span in range(2):
        left = left_ref[first + span]
        for block in range(3):
            keys = spans[span + block]
            if block < 2:
                keys = jnp.where(left >= 2 - block, keys, missing)
            same = jnp.broadcast_to(keys, (128, 128)) == cols[span + 2]
            bias_s[span, :, block * 128 : block * 128 + 128] = jnp.where(same, 0.0, -1e30)

    taken = set()

    def from_pair(shards):
        for key in PAIR:
            if key[:2] in shards and key not in taken:
                taken.add(key)
                rows = rows_of(pair_at(key[0], key[1]), key[2])
                pltpu.make_async_copy(wbuf.at[rows], wbuf.at[rows], pair_sem.at[PAIR[key]]).wait()

    def project(dy):
        from_pair([d for d in SHARDS if dy in d])
        first_block = 3 * lax.rem(y + dy + 4, 4)

        @pl.loop(0, 3)
        def _(j):
            block = first_block + j
            rows = pl.ds(pl.multiple_of(block * 256, 256), 256)

            @pl.when(block < 4)
            def _():
                part = lax.dot_general(
                    normed[ROWS:, :], wbuf[rows, :], (((1,), (1,)), ((), ())), preferred_element_type=jnp.float32
                ).astype(jnp.bfloat16)
                qkv[2 * block, ROWS:, :] = part[:, :128]
                qkv[2 * block + 1, ROWS:, :] = part[:, 128:]

            @pl.when(block >= 4)
            def _():
                part = lax.dot_general(
                    normed[...], wbuf[rows, :], (((1,), (1,)), ((), ())), preferred_element_type=jnp.float32
                ).astype(jnp.bfloat16)
                qkv[2 * block] = part[:, :128]
                qkv[2 * block + 1] = part[:, 128:]

    arrived = set()
    for count, key in enumerate(ARRIVALS, 1):
        d1, d2, piece = key
        rel = (d1, d2)
        owner = seq_at(d1, d2)
        rows = rows_of(owner, piece)
        pltpu.make_async_copy(wbuf.at[rows], wbuf.at[rows], recv_sem.at[RECV[key]]).wait()
        arrived.add(key)
        if d2 == 0:
            if piece == "C":
                if {(1, 0, "C"), (-1, 0, "C")} <= arrived and d1 != 2:
                    forward(seq_at(-turn1, 0), "C", seq_at(turn1, 0), (2, 0, "C"))
            elif d1 == -RELAY[piece]:
                forward(owner, piece, ax1[RELAY[piece]], (2, 0, piece))
            for sign in (1, -1):
                forward(owner, piece, ax2[sign], (d1, -sign, piece))
        elif piece == "C":
            if {(d1, 1, "C"), (d1, -1, "C")} <= arrived and d2 != 2:
                forward(seq_at(d1, -turn2), "C", seq_at(0, turn2), (d1, 2, "C"))
        elif d2 == -RELAY[piece]:
            forward(owner, piece, ax2[RELAY[piece]], (d1, 2, piece))
        if piece == "B":
            to_pair(rel, "B")
        elif rel + ("A",) in arrived and rel + ("C",) in arrived:
            to_pair(rel, "AC")
        if count in FRAME_PARTS:
            send_frames(FRAME_PARTS[count])
        if count == 33:
            for part in range(4):
                rows = pl.ds(part * 64, 64)
                pltpu.make_async_copy(xprev.at[rows], xprev.at[rows], frame_sem.at[part]).wait()
            normed[:ROWS] = layer_norm(xprev[...].astype(jnp.float32)).astype(jnp.bfloat16)
            local[2].wait()
        if count in GROUPS:
            project(GROUPS[count])
    project(2)

    lane = lax.broadcasted_iota(jnp.int32, (128, 128), 1)
    low = lane < 64

    def attend(pair, _):
        for span in range(2):
            q = qkv[pair, ROWS + span * 128 : ROWS + span * 128 + 128, :]
            keys = qkv[NB + pair, span * 128 : span * 128 + 384, :]
            values = qkv[2 * NB + pair, span * 128 : span * 128 + 384, :]
            zero = jnp.zeros_like(q)
            both = jnp.concatenate([jnp.where(low, q, zero), jnp.where(low, zero, q)], axis=0)
            scores = lax.dot_general(
                both, keys, (((1,), (1,)), ((), ())), preferred_element_type=jnp.float32
            )
            mask = bias_s[span]
            scores = scores * (0.125 * LOG2E) + jnp.concatenate([mask, mask], axis=0)
            expo = jnp.exp2(scores - jnp.max(scores, axis=-1, keepdims=True))
            total = jnp.sum(expo, axis=-1, keepdims=True)
            got = jnp.dot(expo.astype(jnp.bfloat16), values, preferred_element_type=jnp.float32)
            got = got / total
            attended[pair, span * 128 : span * 128 + 128, :] = jnp.where(
                low, got[:128], got[128:]
            ).astype(jnp.bfloat16)
        return 0

    lax.fori_loop(0, NB, attend, 0, unroll=4)

    local[1].wait()
    flat = jnp.concatenate([attended[i] for i in range(NB)], axis=1)
    for part in range(4):
        lanes = slice(part * 256, part * 256 + 256)
        cbuf[:, lanes] = (
            xown[:, lanes].astype(jnp.float32)
            + jnp.dot(flat, wo[:, lanes], preferred_element_type=jnp.float32)
        ).astype(jnp.bfloat16)
    cnormed = layer_norm(cbuf[...].astype(jnp.float32)).astype(jnp.bfloat16)
    cedge[0] = cnormed[:16]
    cedge[1] = cnormed[ROWS - 16 :]
    send(cedge.at[0], halo.at[1], halo_sem.at[1], {"seq": prv})
    send(cedge.at[1], halo.at[0], halo_sem.at[0], {"seq": nxt})
    wide = cnormed.astype(jnp.float32)
    for i in range(NB):
        xs[i, 16 : 16 + ROWS, :] = wide[:, i * 128 : i * 128 + 128]
    def convolve(base, tile):
        own = rcol[pl.ds(base + 16, tile), :]
        sums = [jnp.zeros((tile, 128), jnp.float32) for _ in range(NB)]
        for tap in range(TAPS):
            same = rcol[pl.ds(base + tap + 1, tile), :] == own
            for i in range(NB):
                term = dw_ref[tap : tap + 1, i * 128 : i * 128 + 128] * xs[i, pl.ds(base + tap + 1, tile), :]
                sums[i] = sums[i] + jnp.where(same, term, 0.0)
        for i in range(NB):
            lanes = slice(i * 128, i * 128 + 128)
            z = gain_ref[:, lanes] * sums[i] + bias_ref[:, lanes]
            mid = cbuf[pl.ds(base, tile), lanes].astype(jnp.float32)
            out_ref[pl.ds(base, tile), lanes] = (mid + z * jax.nn.sigmoid(z)).astype(jnp.bfloat16)

    @pl.loop(0, 7)
    def _(step):
        convolve(pl.multiple_of(step * 32 + 16, 16), 32)

    for side in range(2):
        pltpu.make_async_copy(halo.at[side], halo.at[side], halo_sem.at[side]).wait()
        wide_halo = halo[side].astype(jnp.float32)
        for i in range(NB):
            xs[i, side * (ROWS + 16) : side * (ROWS + 16) + 16, :] = wide_halo[:, i * 128 : i * 128 + 128]

    @pl.loop(0, 2)
    def _(step):
        convolve(pl.multiple_of(step * (ROWS - 16), 16), 16)

    for copy in sends:
        copy.wait_send()


def on_device(frames, w_qkv, w_out, dw_kernel, conv_gain, conv_bias, rec_ids, left_spans):
    vmem = pl.BlockSpec(memory_space=pltpu.VMEM)
    anyspace = pl.BlockSpec(memory_space=pl.ANY)
    bf = jnp.bfloat16
    return pl.pallas_call(
        kernel,
        out_shape=pltpu.VMEM((ROWS, D), bf),
        in_specs=[anyspace, anyspace, anyspace, vmem, vmem, vmem, vmem,
                  pl.BlockSpec(memory_space=pltpu.SMEM)],
        out_specs=vmem,
        scratch_shapes=[
            pltpu.VMEM((3 * D, D), bf),
            pltpu.VMEM((ROWS, D), bf),
            pltpu.VMEM((ROWS, D), bf),
            pltpu.VMEM((2 * ROWS, D), bf),
            pltpu.VMEM((3 * NB, 2 * ROWS, 128), bf),
            pltpu.VMEM((D, D), bf),
            pltpu.VMEM((NB, ROWS, 128), bf),
            pltpu.VMEM((2, 128, 384), jnp.float32),
            pltpu.VMEM((ROWS, D), bf),
            pltpu.VMEM((2, 16, D), bf),
            pltpu.VMEM((2, 16, D), bf),
            pltpu.VMEM((ROWS + 32, 128), jnp.int32),
            pltpu.VMEM((NB, ROWS + 32, 128), jnp.float32),
            pltpu.SemaphoreType.DMA((3,)),
            pltpu.SemaphoreType.DMA((NSEND,)),
            pltpu.SemaphoreType.DMA((len(ARRIVALS),)),
            pltpu.SemaphoreType.DMA((len(PAIR),)),
            pltpu.SemaphoreType.DMA((4,)),
            pltpu.SemaphoreType.DMA((2,)),
        ],
        compiler_params=pltpu.CompilerParams(
            collective_id=0, has_side_effects=True, vmem_limit_bytes=56 * 1024 * 1024
        ),
    )(
        frames, jnp.transpose(w_qkv), w_out, dw_kernel, conv_gain.reshape(1, D), conv_bias.reshape(1, D),
        rec_ids.reshape(64, 128), left_spans,
    )


def solution(mesh):
    in_specs = (P(("grp", "seq"), None), P(None, "seq"), P(), P(), P(), P(), P("grp"), P("grp"))
    out_specs = P(("grp", "seq"), None)
    return jax.shard_map(
        on_device, mesh=mesh, in_specs=in_specs, out_specs=out_specs, check_vma=False
    )
```
